32 devices in a mesh: row: 16 (over z, y, core), col: 2 (over x).
Axes of the slice: x: 2, y: 2, z: 4, core: 2. Of those that a mesh axis runs over, the one named last changes fastest.
Arguments:
- stiffness: bfloat16 [32, 768, 768], P(('row', 'col'))
- local_inverse: bfloat16 [32, 768, 768], P(('row', 'col'))
- averaging_basis: bfloat16 [32, 768, 64], P(('row', 'col')), may hold values from -0.4375 to 0.4375
- loads: bfloat16 [32, 768, 128], P(('row', 'col')), may hold values from -6 to 6
- start: float32 [6144, 128], P(('row', 'col')), may hold values from -6 to 6
- coarse_inverse: float32 [16, 2, 24, 768], P(None, 'col', None, 'row')
- sizes: int32 [32], P(('row', 'col')), may hold values from 384 to 768, as said below
- dof_ids: int32 [32, 768], P(('row', 'col')), may hold values from 0 to 6143, as said below
- coarse_ids: int32 [32, 64], P(('row', 'col')), may hold values from 0 to 767, as said below
Outputs:
- solution_field: float32 [6144, 128], P(('row', 'col'))
- residual: float32 [6144, 128], P(('row', 'col'))
The draws below stay inside these ranges and needn't reach their ends.
Inputs may be any that keep to these rules, and one draw needn't show every extreme that they name: `sizes`: the largest interface order, 768, occurs in every draw. `dof_ids`: subdomain s sits at row s // 2 and column s % 2; global interface dof g is owned by subdomain g // 192. The 768 slots of a subdomain hold distinct dofs, each owned by the subdomain itself or a subdomain at most one row and one column away; slots from sizes[s] on are not used. `coarse_ids`: coarse dof k is owned by subdomain k // 24. The 64 coarse dofs of a subdomain are distinct, each owned by the subdomain itself or a subdomain at most one row and one column away.
All inputs are finite; a program needn't handle non-finite values.
Results may differ from the reference program's by a relative error of at most 0.0064.
Values may be sent and summed in bfloat16 or wider, within the bound.
A program may use at most 64 MiB of HBM per device.

```python
import jax
import jax.numpy as jnp
from jax import lax

NI = 768
OWN = 192
NP = 64
NCD = 24
COLS = 128
ITERS = 2
GROUPS = 16
MEMBERS = 2
SUBS = 32
NG = 6144
NCO = 768


def square_blocks(key, spread):
    noise = jax.random.normal(key, (SUBS, NI, NI), jnp.float32)
    paired = (noise + jnp.swapaxes(noise, 1, 2)) * (spread / jnp.sqrt(2.0 * NI))
    diagonal = jax.random.uniform(jax.random.fold_in(key, 7), (SUBS, NI), jnp.float32, 0.6, 1.6)
    return paired + diagonal[:, :, None] * jnp.eye(NI, dtype=jnp.float32)[None]


def neighbour_ids(key, per_owner, keep):

    def one_subdomain(index):
        row_here = index // MEMBERS
        col_here = index % MEMBERS
        offsets = jnp.arange(3, dtype=jnp.int32) - 1
        row_list = row_here + offsets[:, None]
        col_list = col_here + offsets[None, :]
        inside = (row_list >= 0) & (row_list < GROUPS) & (col_list >= 0) & (col_list < MEMBERS)
        owner_index = row_list * MEMBERS + col_list
        candidates = (owner_index[:, :, None] * per_owner + jnp.arange(per_owner, dtype=jnp.int32)[None, None, :]).reshape(-1)
        valid = jnp.broadcast_to(inside[:, :, None], (3, 3, per_owner)).reshape(-1)
        shuffled = jax.random.permutation(jax.random.fold_in(key, index), 9 * per_owner).astype(jnp.int32)
        scores = jnp.where(valid, shuffled, shuffled - 9 * per_owner)
        best_scores, picked = lax.top_k(scores, keep)
        return candidates[picked]
    return jax.vmap(one_subdomain)(jnp.arange(SUBS, dtype=jnp.int32))


def draw_stiffness(key, part):
    return square_blocks(jax.random.fold_in(key, 21), 0.4).astype(jnp.bfloat16)


def draw_local_inverse(key, part):
    return square_blocks(jax.random.fold_in(key, 22), 0.5).astype(jnp.bfloat16)


def draw_coarse_inverse(key, part):
    noise = jax.random.normal(jax.random.fold_in(key, 31), (NCO, NCO), jnp.float32) / jnp.sqrt(1.0 * NCO)
    diagonal = jax.random.uniform(jax.random.fold_in(key, 32), (NCO,), jnp.float32, 0.5, 1.5)
    positions = jnp.arange(NCO, dtype=jnp.int32)
    matrix = noise.at[positions, positions].add(diagonal)
    return matrix.T.reshape(GROUPS, MEMBERS, NCD, NCO)


def draw_sizes(key, part):
    values = jax.random.randint(jax.random.fold_in(key, 41), (SUBS,), NI // 2, NI + 1)
    largest = jax.random.randint(jax.random.fold_in(key, 42), (), 0, SUBS)
    return values.at[largest].set(NI).astype(jnp.int32)


def draw_dof_ids(key, part):
    return neighbour_ids(jax.random.fold_in(key, 51), OWN, NI).astype(jnp.int32)


def draw_coarse_ids(key, part):
    return neighbour_ids(jax.random.fold_in(key, 52), NCD, NP).astype(jnp.int32)


def block_levels(key, dims, shards, low, high):
    def one(dim, shards_of):
        draws = jax.random.uniform(jax.random.fold_in(jax.random.fold_in(key, 6), dim), (shards_of,), jnp.float32, low / len(shards), high / len(shards))
        return jnp.repeat(jnp.exp(draws), dims[dim] // shards_of).reshape((-1,) + (1,) * (len(dims) - dim - 1))

    level = one(*shards[0])
    for cut in shards[1:]:
        level = level * one(*cut)
    return level


def bell_draw(own_key, dims, deviation, most, shards=(), kind=jnp.bfloat16):
    entries = deviation * jax.random.normal(own_key, dims, jnp.float32)
    if shards:
        entries = entries * block_levels(own_key, dims, shards, -0.22, 0.18)
    return jnp.clip(entries, -most, most).astype(kind)


def setup_inputs(seed: int = 0) -> dict:
    seeds = jax.random.split(jax.random.key(seed), 10)
    stiffness = draw_stiffness(jax.random.fold_in(seeds[9], 71), 0)
    local_inverse = draw_local_inverse(jax.random.fold_in(seeds[9], 71), 0)
    averaging_basis = bell_draw(seeds[2], (SUBS, NI, NP), (NI // 4) ** -0.5, 0.4375, ((0, 32),))
    loads = bell_draw(seeds[3], (SUBS, NI, COLS), 1.0, 6.0, ((0, 32),))
    start = bell_draw(seeds[4], (NG, COLS), 1.0, 6.0, ((0, 32),), jnp.float32)
    coarse_inverse = draw_coarse_inverse(jax.random.fold_in(seeds[9], 71), 0)
    sizes = draw_sizes(jax.random.fold_in(seeds[9], 71), 0)
    dof_ids = draw_dof_ids(jax.random.fold_in(seeds[9], 71), 0)
    coarse_ids = draw_coarse_ids(jax.random.fold_in(seeds[9], 71), 0)
    return dict(stiffness=stiffness, local_inverse=local_inverse, averaging_basis=averaging_basis, loads=loads, start=start, coarse_inverse=coarse_inverse, sizes=sizes, dof_ids=dof_ids, coarse_ids=coarse_ids)


def apply_each(matrices, vectors):
    return lax.map(lambda operands: jnp.dot(operands[0], operands[1], preferred_element_type=jnp.float32), (matrices, vectors))


def apply_transposed(matrices, vectors):
    return lax.map(lambda operands: jnp.dot(operands[0].T, operands[1], preferred_element_type=jnp.float32), (matrices, vectors))


def reference(stiffness, local_inverse, averaging_basis, loads, start, coarse_inverse, sizes, dof_ids, coarse_ids):
    slots = jnp.arange(NI, dtype=jnp.int32)
    live = slots[None, :] < sizes[:, None]
    live_float = live.astype(jnp.float32)
    target = jnp.where(live, dof_ids, NG).astype(jnp.int32)
    flat_target = target.reshape(-1)
    count = jax.ops.segment_sum(live_float.reshape(-1), flat_target, num_segments=NG + 1)
    weight = live_float / (count[dof_ids] + 1.0 - live_float)
    matrix = coarse_inverse.reshape(NCO, NCO)
    solution_field = start
    residual = start
    for repeat in range(ITERS):
        gathered = solution_field.astype(jnp.bfloat16)[dof_ids]
        local_iterate = jnp.where(live[:, :, None], gathered, jnp.zeros_like(gathered))
        image = apply_each(stiffness, local_iterate)
        terms = loads.astype(jnp.float32) - image
        residual = jax.ops.segment_sum(terms.reshape(-1, COLS), flat_target, num_segments=NG + 1)[:NG]
        scaled = (weight[:, :, None] * residual[dof_ids]).astype(jnp.bfloat16)
        local_part = apply_each(local_inverse, scaled)
        primal = apply_transposed(averaging_basis, scaled)
        coarse_rhs = jax.ops.segment_sum(primal.reshape(-1, COLS), coarse_ids.reshape(-1), num_segments=NCO)
        coarse_solution = jnp.dot(matrix.T, coarse_rhs, precision=lax.Precision.HIGHEST, preferred_element_type=jnp.float32).astype(jnp.bfloat16)
        correction = apply_each(averaging_basis, coarse_solution[coarse_ids])
        update = weight[:, :, None] * (local_part + correction)
        solution_field = solution_field + jax.ops.segment_sum(update.reshape(-1, COLS), flat_target, num_segments=NG + 1)[:NG]
    return solution_field, residual
```

```python
import functools

import jax
import jax.numpy as jnp
from jax import lax
from jax.experimental import pallas as pl
from jax.experimental.pallas import tpu as pltpu
from jax.sharding import PartitionSpec as P

ITERS = 2
BF = jnp.bfloat16
F32 = jnp.float32
MESH_ID = pl.DeviceIdType.MESH
NT = (((1,), (1,)), ((), ()))


def mm(a, b):
    return jnp.dot(a, b, preferred_element_type=F32)


def kernel(
    R, C, B,
    k_hbm, m_hbm, basis_ref, loads_ref, start_ref, panel_ref, sizes_ref, ids_ref, cids_ref,
    x_out, r_out,
    kv, mv, s_ref, st_ref, t_ref, am_ref, a_ref, pbw_ref, bpw_ref, lw_ref,
    idw, xw, rw, psend, precv, usend, urecv, csend, crecv, cw, g_ref, loc_ref, inv_ref,
    ld_sem, s_id, r_id, s_x, r_x, s_r, r_r, s_p, r_p, s_u, r_u, s_c, r_c, s_w, r_w,
    s_g1, r_g1, s_g2, r_g2,
):
    A = R // B
    W = 2 if C == 2 else 3
    NB = 3 * W
    own_k = 0 if W == 2 else 1
    own = W + own_k
    OWN, COLS = start_ref.shape
    NI = ids_ref.shape[1]
    NCD = csend.shape[2]
    r = lax.axis_index("row")
    c = lax.axis_index("col")
    ra = r // B
    rb = r % B

    copy_k = pltpu.make_async_copy(k_hbm, kv, ld_sem.at[0])
    copy_m = pltpu.make_async_copy(m_hbm, mv, ld_sem.at[1])
    copy_k.start()
    copy_m.start()

    def both(x, y):
        if x is None:
            return y
        return x if y is None else jnp.logical_and(x, y)

    def row_ok(d):
        return None if d == 1 else (r > 0 if d == 0 else r < R - 1)

    def col_of(k):
        if W == 2:
            return c if k == 0 else 1 - c
        return c + (k - 1)

    def col_ok(k):
        if W == 2 or k == 1:
            return None
        return c > 0 if k == 0 else c < C - 1

    def mirror(b):
        d, k = b // W, b % W
        return (2 - d) * W + (k if W == 2 else 2 - k)

    nbrs = [b for b in range(NB) if b != own]
    oks = {b: both(row_ok(b // W), col_ok(b % W)) for b in nbrs}
    target = {b: (r + (b // W - 1), col_of(b % W)) for b in nbrs}

    def guarded(ok, fn):
        if ok is None:
            fn()
        else:
            pl.when(ok)(fn)

    def unless(ok, fn):
        if ok is not None:
            pl.when(jnp.logical_not(ok))(fn)

    def remote(src, dst, ss, rs, dev):
        return pltpu.make_async_remote_copy(
            src_ref=src, dst_ref=dst, send_sem=ss, recv_sem=rs,
            device_id=dev, device_id_type=MESH_ID,
        )

    finals = []

    def send_all(make):
        for b in nbrs:
            desc = make(b)
            guarded(oks[b], desc.start)
            finals.append((oks[b], desc.wait_send))

    g1 = [(((ra + i) % A) * B + rb, c) for i in range(A)]
    g2 = {(j, i): (ra * B + (rb + i) % B, (c + j) % C) for j in range(C) for i in range(B)}
    pan = {(d, j): (r + d - 1, (c + j) % C) for d in range(3) for j in range(C) if (d, j) != (1, 0)}

    barrier = pltpu.get_barrier_semaphore()

    def signal(dev):
        pl.semaphore_signal(barrier, inc=1, device_id=dev, device_id_type=MESH_ID)

    for b in nbrs:
        guarded(oks[b], functools.partial(signal, target[b]))
    for i in range(1, A):
        signal(g1[i])
    for key, dev in g2.items():
        if key != (0, 0):
            signal(dev)
    if C > 2:
        for (d, j), dev in pan.items():
            guarded(row_ok(d), functools.partial(signal, dev))

    def floor_div(x, n):
        return jnp.floor((x + 0.5) * (1.0 / n))

    ids_i = ids_ref[...]
    live = lax.broadcasted_iota(jnp.int32, (1, NI), 1) < sizes_ref[0]
    idw[own] = jnp.where(live, ids_i, -1)
    ids_f = ids_i.astype(F32)
    owner = floor_div(ids_f, OWN)
    orow = floor_div(owner, C)
    ocol = owner - orow * C
    rf = r.astype(F32)
    cf = c.astype(F32)
    kslot = jnp.abs(ocol - cf) if W == 2 else ocol - cf + 1.0
    pos_f = ((orow - rf + 1.0) * W + kslot) * OWN + (ids_f - owner * OWN)
    pos = jnp.where(live, pos_f, -1.0).astype(jnp.int32)
    xw[0, own] = start_ref[...].astype(BF)

    for b in nbrs:
        def fill(b=b):
            idw[b] = jnp.full((1, NI), -1, jnp.int32)
            for s in range(ITERS):
                xw[s, b] = jnp.zeros((OWN, COLS), BF)
                rw[s, b] = jnp.zeros((OWN, COLS), BF)
        unless(oks[b], fill)
    for d in (0, 2):
        def fill_c(d=d):
            for j in range(C):
                cw[j, d] = jnp.zeros(cw.shape[2:], BF)
        unless(row_ok(d), fill_c)
    cw[c, 1] = panel_ref[...]

    amount = (A - 1) + (C * B - 1)
    conds = [oks[b] for b in nbrs]
    if C > 2:
        conds += [row_ok(d) for d, j in pan]
    for ok in conds:
        amount = amount + (1 if ok is None else ok.astype(jnp.int32))
    pl.semaphore_wait(barrier, amount)

    def send_x(s):
        send_all(lambda b: remote(
            xw.at[s, own], xw.at[s, mirror(b)], s_x.at[s, b], r_x.at[s, mirror(b)], target[b]))

    send_x(0)
    send_all(lambda b: remote(
        idw.at[own], idw.at[mirror(b)], s_id.at[b], r_id.at[mirror(b)], target[b]))

    pos_col = jnp.transpose(jnp.broadcast_to(pos, (128, NI)))
    WN = NB * OWN
    for j in range(0, WN, 128):
        n = min(128, WN - j)
        lane = lax.broadcasted_iota(jnp.int32, (NI, 128), 1) + j
        hot = jnp.where(lane == pos_col, 1.0, 0.0).astype(BF)
        s_ref[:, j:j + n] = hot[:, :n]
    for b in range(NB):
        sub = lax.broadcasted_iota(jnp.int32, (OWN, NI), 0) + b * OWN
        st_ref[b * OWN:(b + 1) * OWN, :] = jnp.where(sub == pos, 1.0, 0.0).astype(BF)

    def by_rows(rows, fn):
        def step(i, carry):
            fn(pl.ds(pl.multiple_of(i * OWN, OWN), OWN))
            return carry
        lax.fori_loop(0, rows // OWN, step, 0)

    def times_s(src, dst):
        def one(at):
            dst[at, :] = mm(src[at, :], s_ref[...]).astype(BF)
        by_rows(NI, one)

    def st_times(src, dst):
        def one(at):
            dst[at, :] = mm(st_ref[at, :], src[...]).astype(dst.dtype)
        by_rows(WN, one)

    def recv(dst, sem):
        return remote(dst, dst, sem, sem, (r, c)).wait_recv

    copy_k.wait()
    times_s(kv, t_ref)
    st_times(loads_ref, lw_ref)
    st_times(t_ref, a_ref)

    inv = None
    x_now = start_ref[...]
    for s in range(ITERS):
        for b in nbrs:
            guarded(oks[b], recv(xw.at[s, b], r_x.at[s, b]))
        x_all = xw[s].reshape(WN, COLS)
        for b in nbrs + [own]:
            at = slice(b * OWN, (b + 1) * OWN)
            part = lw_ref[at, :].astype(F32) - mm(a_ref[at, :], x_all)
            if b == own:
                r_out[...] = part
            else:
                psend[s, b] = part.astype(BF)
                desc = remote(psend.at[s, b], precv.at[s, mirror(b)], s_p.at[s, b],
                              r_p.at[s, mirror(b)], target[b])
                guarded(oks[b], desc.start)
                finals.append((oks[b], desc.wait_send))
        if s == 0:
            for (d, j), dev in pan.items():
                desc = remote(panel_ref, cw.at[c, 2 - d], s_w.at[d, j], r_w.at[2 - d, j], dev)
                guarded(row_ok(d), desc.start)
                finals.append((row_ok(d), desc.wait_send))
            for b in nbrs:
                guarded(oks[b], recv(idw.at[b], r_id.at[b]))
            mine = lax.broadcasted_iota(jnp.int32, (OWN, 128), 0) + (r * C + c) * OWN
            acc = jnp.zeros((OWN, 128), F32)
            for b in range(NB):
                for j in range(0, NI, 128):
                    acc = acc + jnp.where(idw[b, :, j:j + 128] == mine, 1.0, 0.0)
            count = jnp.sum(acc, axis=1, keepdims=True)
            inv_ref[...] = jnp.broadcast_to(1.0 / jnp.maximum(count, 1.0), (OWN, COLS))

            cf_ids = cids_ref[...].astype(F32)
            cpos = (cf_ids - (rf - 1.0) * (C * NCD)).astype(jnp.int32)
            n_c = 3 * C * NCD
            pt = jnp.where(
                lax.broadcasted_iota(jnp.int32, (n_c, cpos.shape[1]), 0) == cpos, 1.0, 0.0
            ).astype(BF)
            basis = basis_ref[...]
            pb = lax.dot_general(pt, basis, NT, preferred_element_type=F32).astype(BF)
            bp = lax.dot_general(basis, pt, NT, preferred_element_type=F32).astype(BF)
            pbw_ref[...] = mm(pb, s_ref[...]).astype(BF)
            by_rows(WN, lambda at: bpw_ref.__setitem__((at, slice(None)), mm(st_ref[at, :], bp).astype(BF)))
            copy_m.wait()
            times_s(mv, t_ref)
        for b in nbrs:
            guarded(oks[b], recv(precv.at[s, b], r_p.at[s, b]))

            def add(b=b):
                r_out[...] = r_out[...] + precv[s, b].astype(F32)
            guarded(oks[b], add)
        rw[s, own] = (inv_ref[...] * r_out[...]).astype(BF)
        send_all(lambda b: remote(
            rw.at[s, own], rw.at[s, mirror(b)], s_r.at[s, b], r_r.at[s, mirror(b)], target[b]))
        if s == 0:
            st_times(t_ref, am_ref)
        for b in nbrs:
            guarded(oks[b], recv(rw.at[s, b], r_r.at[s, b]))
        r_all = rw[s].reshape(WN, COLS)
        csend[s] = mm(pbw_ref[...], r_all).reshape(csend.shape[1:])
        send_all(lambda b: remote(
            csend.at[s, (b // W) * C + target[b][1]], crecv.at[s, mirror(b)],
            s_c.at[s, b], r_c.at[s, mirror(b)], target[b]))
        crecv[s, own] = csend[s, C + c]

        def local(at):
            loc_ref[at, :] = mm(am_ref[at, :], rw[s].reshape(WN, COLS))
        by_rows(WN, local)
        for b in nbrs:
            guarded(oks[b], recv(crecv.at[s, b], r_c.at[s, b]))

            def add_c(b=b):
                crecv[s, own] = crecv[s, own] + crecv[s, b]
            guarded(oks[b], add_c)
        g_ref[s, c, rb, ra] = crecv[s, own].astype(BF)
        for i in range(1, A):
            at = g_ref.at[s, c, rb, ra]
            desc = remote(at, at, s_g1.at[s, i], r_g1.at[s, i], g1[i])
            desc.start()
            finals.append((None, desc.wait_send))
        for i in range(1, A):
            recv(g_ref.at[s, c, rb, (ra + A - i) % A], r_g1.at[s, i])()
        for (j, i), dev in g2.items():
            if (j, i) == (0, 0):
                continue
            at = g_ref.at[s, c, rb]
            desc = remote(at, at, s_g2.at[s, j, i], r_g2.at[s, j, i], dev)
            desc.start()
            finals.append((None, desc.wait_send))
        for (j, i) in g2:
            if (j, i) == (0, 0):
                continue
            recv(g_ref.at[s, (c + C - j) % C, (rb + B - i) % B], r_g2.at[s, j, i])()
        if s == 0:
            for (d, j) in pan:
                guarded(row_ok(d), recv(cw.at[(c + C - j) % C, d], r_w.at[d, j]))
        sol = None
        for j in range(C):
            rhs = g_ref[s, j].astype(F32).reshape(R * NCD, COLS).astype(BF)
            term = mm(cw[j].reshape(3 * cw.shape[2], R * NCD), rhs)
            sol = term if sol is None else sol + term
        sol = sol.astype(BF)
        x_out[...] = x_now
        for b in nbrs + [own]:
            at = slice(b * OWN, (b + 1) * OWN)
            upd = loc_ref[at, :] + mm(bpw_ref[at, :], sol)
            if b == own:
                loc_ref[at, :] = upd
            else:
                usend[s, b] = upd.astype(BF)
                desc = remote(usend.at[s, b], urecv.at[s, mirror(b)], s_u.at[s, b],
                              r_u.at[s, mirror(b)], target[b])
                guarded(oks[b], desc.start)
                finals.append((oks[b], desc.wait_send))
        mine_at = slice(own * OWN, (own + 1) * OWN)
        for b in nbrs:
            guarded(oks[b], recv(urecv.at[s, b], r_u.at[s, b]))

            def add_u(b=b):
                loc_ref[mine_at, :] = loc_ref[mine_at, :] + urecv[s, b].astype(F32)
            guarded(oks[b], add_u)
        x_now = x_out[...] + inv_ref[...] * loc_ref[mine_at, :]
        x_out[...] = x_now
        if s + 1 < ITERS:
            xw[s + 1, own] = x_now.astype(BF)
            send_x(s + 1)
    for ok, fn in finals:
        guarded(ok, fn)


def solution(mesh):
    R, C = mesh.shape["row"], mesh.shape["col"]
    B = 4 if R % 4 == 0 else (2 if R % 2 == 0 else 1)
    A = R // B
    W = 2 if C == 2 else 3
    NB = 3 * W

    def body(stiffness, local_inverse, averaging_basis, loads, start, coarse_inverse, sizes,
             dof_ids, coarse_ids):
        OWN, COLS = start.shape
        NI = dof_ids.shape[1]
        NCD, NR = coarse_inverse.shape[2:]
        WN = NB * OWN
        panel = coarse_inverse.reshape(A, B, NCD, NR).transpose(3, 1, 0, 2)
        panel = panel.reshape(NR, R * NCD).astype(BF)
        V = pltpu.VMEM
        D = pltpu.SemaphoreType.DMA
        S = ITERS
        vm = pl.BlockSpec(memory_space=pltpu.VMEM)
        hb = pl.BlockSpec(memory_space=pl.ANY)
        sm = pl.BlockSpec(memory_space=pltpu.SMEM)
        n_c = 3 * C * NCD
        return pl.pallas_call(
            functools.partial(kernel, R, C, B),
            out_shape=(jax.ShapeDtypeStruct((OWN, COLS), F32),) * 2,
            in_specs=[hb, hb, vm, vm, vm, vm, sm, vm, vm],
            out_specs=(vm, vm),
            scratch_shapes=[
                V((NI, NI), BF), V((NI, NI), BF), V((NI, WN), BF), V((WN, NI), BF),
                V((NI, WN), BF), V((WN, WN), BF), V((WN, WN), BF),
                V((n_c, WN), BF), V((WN, n_c), BF), V((WN, COLS), BF),
                V((NB, 1, NI), jnp.int32), V((S, NB, OWN, COLS), BF), V((S, NB, OWN, COLS), BF),
                V((S, NB, OWN, COLS), BF), V((S, NB, OWN, COLS), BF),
                V((S, NB, OWN, COLS), BF), V((S, NB, OWN, COLS), BF),
                V((S, 3 * C, NCD, COLS), F32), V((S, NB, NCD, COLS), F32),
                V((C, 3, NR, R * NCD), BF), V((S, C, B, A, NCD, COLS), BF),
                V((WN, COLS), F32), V((OWN, COLS), F32),
                D((2,)), D((NB,)), D((NB,)), D((S, NB)), D((S, NB)), D((S, NB)), D((S, NB)),
                D((S, NB)), D((S, NB)), D((S, NB)), D((S, NB)), D((S, NB)), D((S, NB)),
                D((3, C)), D((3, C)), D((S, A)), D((S, A)), D((S, C, B)), D((S, C, B)),
            ],
            compiler_params=pltpu.CompilerParams(
                collective_id=0, has_side_effects=True, vmem_limit_bytes=62 << 20
            ),
        )(stiffness[0], local_inverse[0], averaging_basis[0], loads[0], start, panel, sizes,
          dof_ids, coarse_ids)

    in_specs = (
        P(("row", "col"), None, None),
        P(("row", "col"), None, None),
        P(("row", "col"), None, None),
        P(("row", "col"), None, None),
        P(("row", "col"), None),
        P(None, "col", None, "row"),
        P(("row", "col")),
        P(("row", "col"), None),
        P(("row", "col"), None),
    )
    out_specs = (P(("row", "col"), None), P(("row", "col"), None))
    return jax.shard_map(body, mesh=mesh, in_specs=in_specs, out_specs=out_specs, check_vma=False)
```

```python
import functools

import jax
import jax.numpy as jnp
from jax import lax
from jax.experimental import pallas as pl
from jax.experimental.pallas import tpu as pltpu
from jax.sharding import PartitionSpec as P

ITERS = 2
BF = jnp.bfloat16
F32 = jnp.float32
MESH_ID = pl.DeviceIdType.MESH
NT = (((1,), (1,)), ((), ()))


def mm(a, b):
    return jnp.dot(a, b, preferred_element_type=F32)


def kernel(
    R, C, B,
    k_hbm, m_hbm, basis_ref, loads_ref, start_ref, panel_ref, sizes_ref, ids_ref, cids_ref,
    x_out, r_out,
    kv, mv, s_ref, st_ref, t_ref, t2_ref, tv_ref, tl_ref, pbs, pbr, qt,
    idw, xw, rw, psend, precv, usend, urecv, csend, crecv, cw, pan_ref, g_ref, inv_ref, acc_ref,
    ld_sem, s_id, r_id, s_x, r_x, s_r, r_r, s_p, r_p, s_u, r_u, s_b, r_b, s_c, r_c, s_w, r_w,
    s_g1, r_g1, s_g2, r_g2,
):
    A = R // B
    W = 2 if C == 2 else 3
    NB = 3 * W
    own_k = 0 if W == 2 else 1
    own = W + own_k
    OWN, COLS = start_ref.shape
    NI = ids_ref.shape[1]
    NCD, NR = panel_ref.shape[1:]
    n_c = 3 * NR
    r = lax.axis_index("row")
    c = lax.axis_index("col")
    ra = r // B
    rb = r % B

    copy_k = pltpu.make_async_copy(k_hbm, kv, ld_sem.at[0])
    copy_m = pltpu.make_async_copy(m_hbm, mv, ld_sem.at[1])
    copy_k.start()
    copy_m.start()

    def both(x, y):
        if x is None:
            return y
        return x if y is None else jnp.logical_and(x, y)

    def row_ok(d):
        return None if d == 1 else (r > 0 if d == 0 else r < R - 1)

    def row_ok5(e):
        if e == 2:
            return None
        return r >= 2 - e if e < 2 else r < R - (e - 2)

    def col_of(k):
        if W == 2:
            return c if k == 0 else 1 - c
        return c + (k - 1)

    def col_ok(k):
        if W == 2 or k == 1:
            return None
        return c > 0 if k == 0 else c < C - 1

    def mirror(b):
        d, k = b // W, b % W
        return (2 - d) * W + (k if W == 2 else 2 - k)

    nbrs = [b for b in range(NB) if b != own]
    oks = {b: both(row_ok(b // W), col_ok(b % W)) for b in nbrs}
    target = {b: (r + (b // W - 1), col_of(b % W)) for b in nbrs}

    def guarded(ok, fn):
        if ok is None:
            fn()
        else:
            pl.when(ok)(fn)

    def unless(ok, fn):
        if ok is not None:
            pl.when(jnp.logical_not(ok))(fn)

    def remote(src, dst, ss, rs, dev):
        return pltpu.make_async_remote_copy(
            src_ref=src, dst_ref=dst, send_sem=ss, recv_sem=rs,
            device_id=dev, device_id_type=MESH_ID,
        )

    finals = []

    def send_all(make):
        for b in nbrs:
            desc = make(b)
            guarded(oks[b], desc.start)
            finals.append((oks[b], desc.wait_send))

    g1 = [(((ra + i) % A) * B + rb, c) for i in range(A)]
    g2 = {(j, i): (ra * B + (rb + i) % B, (c + j) % C) for j in range(C) for i in range(B)}
    far = {(e, j): (r + (e - 2), (c + j) % C) for e in range(5) for j in range(C)
           if (e, j) != (2, 0)}

    barrier = pltpu.get_barrier_semaphore()

    def signal(dev):
        pl.semaphore_signal(barrier, inc=1, device_id=dev, device_id_type=MESH_ID)

    for (e, j), dev in far.items():
        guarded(row_ok5(e), functools.partial(signal, dev))
    for i in range(1, A):
        signal(g1[i])
    for key, dev in g2.items():
        if key != (0, 0):
            signal(dev)

    def floor_div(x, n):
        return jnp.floor((x + 0.5) * (1.0 / n))

    ids_i = ids_ref[...]
    live = lax.broadcasted_iota(jnp.int32, (1, NI), 1) < sizes_ref[0]
    idw[own] = jnp.where(live, ids_i, -1)
    ids_f = ids_i.astype(F32)
    owner = floor_div(ids_f, OWN)
    orow = floor_div(owner, C)
    ocol = owner - orow * C
    rf = r.astype(F32)
    cf = c.astype(F32)
    kslot = jnp.abs(ocol - cf) if W == 2 else ocol - cf + 1.0
    pos_f = ((orow - rf + 1.0) * W + kslot) * OWN + (ids_f - owner * OWN)
    pos = jnp.where(live, pos_f, -1.0).astype(jnp.int32)
    xw[0, own] = start_ref[...].astype(BF)

    for b in nbrs:
        def fill(b=b):
            idw[b] = jnp.full((1, NI), -1, jnp.int32)
            for s in range(ITERS):
                xw[s, b] = jnp.zeros((OWN, COLS), BF)
                rw[s, b] = jnp.zeros((OWN, COLS), BF)
            pbr[b] = jnp.zeros((n_c, OWN), BF)
        unless(oks[b], fill)
    for e in (0, 1, 3, 4):
        def fill_c(e=e):
            for j in range(C):
                cw[j, e] = jnp.zeros(cw.shape[2:], BF)
        unless(row_ok5(e), fill_c)

    amount = (A - 1) + (C * B - 1)
    for e, j in far:
        ok = row_ok5(e)
        amount = amount + (1 if ok is None else ok.astype(jnp.int32))
    pl.semaphore_wait(barrier, amount)

    def send_x(s):
        send_all(lambda b: remote(
            xw.at[s, own], xw.at[s, mirror(b)], s_x.at[s, b], r_x.at[s, mirror(b)], target[b]))

    send_x(0)
    send_all(lambda b: remote(
        idw.at[own], idw.at[mirror(b)], s_id.at[b], r_id.at[mirror(b)], target[b]))

    pos_col = jnp.transpose(jnp.broadcast_to(pos, (128, NI)))
    WN = NB * OWN
    for j in range(0, WN, 128):
        n = min(128, WN - j)
        lane = lax.broadcasted_iota(jnp.int32, (NI, 128), 1) + j
        hot = jnp.where(lane == pos_col, 1.0, 0.0).astype(BF)
        s_ref[:, j:j + n] = hot[:, :n]
    for b in range(NB):
        sub = lax.broadcasted_iota(jnp.int32, (OWN, NI), 0) + b * OWN
        st_ref[b * OWN:(b + 1) * OWN, :] = jnp.where(sub == pos, 1.0, 0.0).astype(BF)

    def by_rows(rows, fn):
        def step(i, carry):
            fn(pl.ds(pl.multiple_of(i * OWN, OWN), OWN))
            return carry
        lax.fori_loop(0, rows // OWN, step, 0)

    def times_s(src, dst):
        def one(at):
            dst[at, :] = mm(src[at, :], s_ref[...]).astype(BF)
        by_rows(NI, one)

    def recv(dst, sem):
        return remote(dst, dst, sem, sem, (r, c)).wait_recv

    def rows_of(b):
        return slice(b * OWN, (b + 1) * OWN)

    def scatter(value, send, land, ss, rs, s):
        tv_ref[...] = value.astype(BF)
        for b in nbrs:
            send[s, b] = mm(st_ref[rows_of(b), :], tv_ref[...]).astype(BF)
            desc = remote(send.at[s, b], land.at[s, mirror(b)], ss.at[s, b],
                          rs.at[s, mirror(b)], target[b])
            guarded(oks[b], desc.start)
            finals.append((oks[b], desc.wait_send))
        tl_ref[...] = (value - tv_ref[...].astype(F32)).astype(BF)
        mine = st_ref[rows_of(own), :]
        return mm(mine, tv_ref[...]) + mm(mine, tl_ref[...])

    cpos = (cids_ref[...].astype(F32) - (rf - 1.0) * NR).astype(jnp.int32)
    pt = jnp.where(
        lax.broadcasted_iota(jnp.int32, (n_c, cpos.shape[1]), 0) == cpos, 1.0, 0.0
    ).astype(BF)
    pb = mm(pt, basis_ref[...]).astype(BF)
    for b in nbrs + [own]:
        block = lax.dot_general(pb, st_ref[rows_of(b), :], NT, preferred_element_type=F32)
        if b == own:
            pbr[own] = block.astype(BF)
        else:
            pbs[b] = block.astype(BF)
            desc = remote(pbs.at[b], pbr.at[mirror(b)], s_b.at[b], r_b.at[mirror(b)], target[b])
            guarded(oks[b], desc.start)
            finals.append((oks[b], desc.wait_send))

    copy_k.wait()
    times_s(kv, t_ref)

    for s in range(ITERS):
        for b in nbrs:
            guarded(oks[b], recv(xw.at[s, b], r_x.at[s, b]))
        terms = loads_ref[...].astype(F32) - mm(t_ref[...], xw[s].reshape(WN, COLS))
        r_out[...] = scatter(terms, psend, precv, s_p, r_p, s)
        if s == 0:
            flat = jnp.concatenate(
                [panel_ref[a * B + b] for b in range(B) for a in range(A)], axis=0)
            pan_ref[...] = jnp.transpose(flat).astype(BF)
            cw[c, 2] = pan_ref[...]
            for (e, j), dev in far.items():
                desc = remote(pan_ref, cw.at[c, 4 - e], s_w.at[e, j], r_w.at[4 - e, j], dev)
                guarded(row_ok5(e), desc.start)
                finals.append((row_ok5(e), desc.wait_send))
            for b in nbrs:
                guarded(oks[b], recv(idw.at[b], r_id.at[b]))
            mine = lax.broadcasted_iota(jnp.int32, (OWN, 128), 0) + (r * C + c) * OWN
            acc = jnp.zeros((OWN, 128), F32)
            for b in range(NB):
                for j in range(0, NI, 128):
                    acc = acc + jnp.where(idw[b, :, j:j + 128] == mine, 1.0, 0.0)
            count = jnp.sum(acc, axis=1, keepdims=True)
            inv_ref[...] = jnp.broadcast_to(1.0 / jnp.maximum(count, 1.0), (OWN, COLS))
            copy_m.wait()
            times_s(mv, t2_ref)
            for b in nbrs:
                guarded(oks[b], recv(pbr.at[b], r_b.at[b]))
            for b in range(NB):
                qt[b] = jnp.transpose(pbr[b].astype(F32)).astype(BF)
        for b in nbrs:
            guarded(oks[b], recv(precv.at[s, b], r_p.at[s, b]))

            def add(b=b):
                r_out[...] = r_out[...] + precv[s, b].astype(F32)
            guarded(oks[b], add)
        z = (inv_ref[...] * r_out[...]).astype(BF)
        rw[s, own] = z
        bands = [None] * 5
        for b in range(NB):
            part = mm(pbr[b], z).reshape(3, C, NCD, COLS)
            for dd in range(3):
                e = b // W + dd
                bands[e] = part[dd] if bands[e] is None else bands[e] + part[dd]
        for e in range(5):
            csend[s, e * C:(e + 1) * C] = bands[e]
        for (e, j), dev in far.items():
            desc = remote(csend.at[s, e * C + dev[1]], crecv.at[s, 4 - e, j],
                          s_c.at[s, e, j], r_c.at[s, 4 - e, j], dev)
            guarded(row_ok5(e), desc.start)
            finals.append((row_ok5(e), desc.wait_send))
        send_all(lambda b: remote(
            rw.at[s, own], rw.at[s, mirror(b)], s_r.at[s, b], r_r.at[s, mirror(b)], target[b]))
        crecv[s, 2, 0] = csend[s, 2 * C + c]
        for e, j in far:
            guarded(row_ok5(e), recv(crecv.at[s, e, j], r_c.at[s, e, j]))

            def add_c(e=e, j=j):
                crecv[s, 2, 0] = crecv[s, 2, 0] + crecv[s, e, j]
            guarded(row_ok5(e), add_c)
        g_ref[s, c, rb, ra] = crecv[s, 2, 0].astype(BF)
        for i in range(1, A):
            at = g_ref.at[s, c, rb, ra]
            desc = remote(at, at, s_g1.at[s, i], r_g1.at[s, i], g1[i])
            desc.start()
            finals.append((None, desc.wait_send))
        for b in nbrs:
            guarded(oks[b], recv(rw.at[s, b], r_r.at[s, b]))
        acc_ref[...] = scatter(
            mm(t2_ref[...], rw[s].reshape(WN, COLS)), usend, urecv, s_u, r_u, s)
        for i in range(1, A):
            recv(g_ref.at[s, c, rb, (ra + A - i) % A], r_g1.at[s, i])()
        for (j, i), dev in g2.items():
            if (j, i) == (0, 0):
                continue
            at = g_ref.at[s, c, rb]
            desc = remote(at, at, s_g2.at[s, j, i], r_g2.at[s, j, i], dev)
            desc.start()
            finals.append((None, desc.wait_send))
        for (j, i) in g2:
            if (j, i) == (0, 0):
                continue
            recv(g_ref.at[s, (c + C - j) % C, (rb + B - i) % B], r_g2.at[s, j, i])()
        if s == 0:
            for e, j in far:
                guarded(row_ok5(e), recv(cw.at[(c + C - j) % C, e], r_w.at[e, j]))
        sol = None
        for j in range(C):
            rhs = g_ref[s, j].astype(F32).reshape(R * NCD, COLS).astype(BF)
            term = mm(cw[j].reshape(5 * NR, R * NCD), rhs)
            sol = term if sol is None else sol + term
        sol = sol.astype(BF)
        total = acc_ref[...]
        for b in range(NB):
            d = b // W
            total = total + mm(qt[b], sol[d * NR:(d + 3) * NR])
        acc_ref[...] = total
        for b in nbrs:
            guarded(oks[b], recv(urecv.at[s, b], r_u.at[s, b]))

            def add_u(b=b):
                acc_ref[...] = acc_ref[...] + urecv[s, b].astype(F32)
            guarded(oks[b], add_u)
        x_now = (start_ref if s == 0 else x_out)[...] + inv_ref[...] * acc_ref[...]
        x_out[...] = x_now
        if s + 1 < ITERS:
            xw[s + 1, own] = x_now.astype(BF)
            send_x(s + 1)
    for ok, fn in finals:
        guarded(ok, fn)


def solution(mesh):
    R, C = mesh.shape["row"], mesh.shape["col"]
    B = 4 if R % 4 == 0 else (2 if R % 2 == 0 else 1)
    A = R // B
    W = 2 if C == 2 else 3
    NB = 3 * W

    def body(stiffness, local_inverse, averaging_basis, loads, start, coarse_inverse, sizes,
             dof_ids, coarse_ids):
        OWN, COLS = start.shape
        NI = dof_ids.shape[1]
        NCD, NR = coarse_inverse.shape[2:]
        WN = NB * OWN
        panel = coarse_inverse.reshape(R, NCD, NR)
        V = pltpu.VMEM
        D = pltpu.SemaphoreType.DMA
        S = ITERS
        vm = pl.BlockSpec(memory_space=pltpu.VMEM)
        hb = pl.BlockSpec(memory_space=pl.ANY)
        sm = pl.BlockSpec(memory_space=pltpu.SMEM)
        n_c = 3 * NR
        return pl.pallas_call(
            functools.partial(kernel, R, C, B),
            out_shape=(jax.ShapeDtypeStruct((OWN, COLS), F32),) * 2,
            in_specs=[hb, hb, vm, vm, vm, vm, sm, vm, vm],
            out_specs=(vm, vm),
            scratch_shapes=[
                V((NI, NI), BF), V((NI, NI), BF), V((NI, WN), BF), V((WN, NI), BF),
                V((NI, WN), BF), V((NI, WN), BF), V((NI, COLS), BF), V((NI, COLS), BF),
                V((NB, n_c, OWN), BF), V((NB, n_c, OWN), BF), V((NB, OWN, n_c), BF),
                V((NB, 1, NI), jnp.int32), V((S, NB, OWN, COLS), BF), V((S, NB, OWN, COLS), BF),
                V((S, NB, OWN, COLS), BF), V((S, NB, OWN, COLS), BF),
                V((S, NB, OWN, COLS), BF), V((S, NB, OWN, COLS), BF),
                V((S, 5 * C, NCD, COLS), F32), V((S, 5, C, NCD, COLS), F32),
                V((C, 5, NR, R * NCD), BF), V((NR, R * NCD), BF),
                V((S, C, B, A, NCD, COLS), BF),
                V((OWN, COLS), F32), V((OWN, COLS), F32),
                D((2,)), D((NB,)), D((NB,)), D((S, NB)), D((S, NB)), D((S, NB)), D((S, NB)),
                D((S, NB)), D((S, NB)), D((S, NB)), D((S, NB)), D((NB,)), D((NB,)),
                D((S, 5, C)), D((S, 5, C)), D((5, C)), D((5, C)),
                D((S, A)), D((S, A)), D((S, C, B)), D((S, C, B)),
            ],
            compiler_params=pltpu.CompilerParams(
                collective_id=0, has_side_effects=True, vmem_limit_bytes=62 << 20
            ),
        )(stiffness[0], local_inverse[0], jnp.swapaxes(averaging_basis[0], 0, 1), loads[0], start, panel, sizes,
          dof_ids, coarse_ids)

    in_specs = (
        P(("row", "col"), None, None),
        P(("row", "col"), None, None),
        P(("row", "col"), None, None),
        P(("row", "col"), None, None),
        P(("row", "col"), None),
        P(None, "col", None, "row"),
        P(("row", "col")),
        P(("row", "col"), None),
        P(("row", "col"), None),
    )
    out_specs = (P(("row", "col"), None), P(("row", "col"), None))
    return jax.shard_map(body, mesh=mesh, in_specs=in_specs, out_specs=out_specs, check_vma=False)
```

```python
import functools

import jax
import jax.numpy as jnp
from jax import lax
from jax.experimental import pallas as pl
from jax.experimental.pallas import tpu as pltpu
from jax.sharding import PartitionSpec as P

ITERS = 2
BF = jnp.bfloat16
F32 = jnp.float32
MESH_ID = pl.DeviceIdType.MESH
NT = (((1,), (1,)), ((), ()))


def mm(a, b):
    return jnp.dot(a, b, preferred_element_type=F32)


def kernel(
    R, C, B,
    k_hbm, m_hbm, basis_ref, loads_ref, start_ref, panel_ref, sizes_ref, ids_ref, cids_ref,
    x_out, r_out,
    kv, mv, s_ref, st_ref, t_ref, t2_ref, tv_ref, tl_ref, pbs, pbl, pbr, qt,
    idw, xw, rw, psend, precv, usend, urecv, csend, crecv, cw, pan_ref, g_ref, inv_ref, acc_ref,
    ld_sem, s_id, r_id, s_x, r_x, s_r, r_r, s_p, r_p, s_u, r_u, s_b, r_b, s_c, r_c, s_w, r_w,
    s_g1, r_g1, s_g2, r_g2,
):
    A = R // B
    W = 2 if C == 2 else 3
    NB = 3 * W
    own_k = 0 if W == 2 else 1
    own = W + own_k
    OWN, COLS = start_ref.shape
    NI = ids_ref.shape[1]
    NCD, NR = panel_ref.shape[1:]
    n_c = 3 * NR
    r = lax.axis_index("row")
    c = lax.axis_index("col")
    ra = r // B
    rb = r % B

    copy_k = pltpu.make_async_copy(k_hbm, kv, ld_sem.at[0])
    copy_m = pltpu.make_async_copy(m_hbm, mv, ld_sem.at[1])
    copy_k.start()
    copy_m.start()

    def both(x, y):
        if x is None:
            return y
        return x if y is None else jnp.logical_and(x, y)

    def row_ok(d):
        return None if d == 1 else (r > 0 if d == 0 else r < R - 1)

    def row_ok5(e):
        if e == 2:
            return None
        return r >= 2 - e if e < 2 else r < R - (e - 2)

    def col_of(k):
        if W == 2:
            return c if k == 0 else 1 - c
        return c + (k - 1)

    def col_ok(k):
        if W == 2 or k == 1:
            return None
        return c > 0 if k == 0 else c < C - 1

    def mirror(b):
        d, k = b // W, b % W
        return (2 - d) * W + (k if W == 2 else 2 - k)

    nbrs = sorted((b for b in range(NB) if b != own), key=lambda b: (b % W == own_k, b // W == 1))
    oks = {b: both(row_ok(b // W), col_ok(b % W)) for b in nbrs}
    target = {b: (r + (b // W - 1), col_of(b % W)) for b in nbrs}

    def guarded(ok, fn):
        if ok is None:
            fn()
        else:
            pl.when(ok)(fn)

    def unless(ok, fn):
        if ok is not None:
            pl.when(jnp.logical_not(ok))(fn)

    def remote(src, dst, ss, rs, dev):
        return pltpu.make_async_remote_copy(
            src_ref=src, dst_ref=dst, send_sem=ss, recv_sem=rs,
            device_id=dev, device_id_type=MESH_ID,
        )

    finals = []

    def send_all(make):
        for b in nbrs:
            desc = make(b)
            guarded(oks[b], desc.start)
            finals.append((oks[b], desc.wait_send))

    g1 = [(((ra + i) % A) * B + rb, c) for i in range(A)]
    g2 = {(j, i): (ra * B + (rb + i) % B, (c + j) % C) for j in range(C) for i in range(B)}
    far = {(e, j): (r + (e - 2), (c + j) % C) for e in range(5) for j in range(C)
           if (e, j) != (2, 0)}

    barrier = pltpu.get_barrier_semaphore()

    def signal(dev):
        pl.semaphore_signal(barrier, inc=1, device_id=dev, device_id_type=MESH_ID)

    for (e, j), dev in far.items():
        guarded(row_ok5(e), functools.partial(signal, dev))
    for i in range(1, A):
        signal(g1[i])
    for key, dev in g2.items():
        if key != (0, 0):
            signal(dev)

    def floor_div(x, n):
        return jnp.floor((x + 0.5) * (1.0 / n))

    ids_i = ids_ref[...]
    live = lax.broadcasted_iota(jnp.int32, (1, NI), 1) < sizes_ref[0]
    idw[own, :, :NI] = jnp.where(live, ids_i, -1)
    NP = cids_ref.shape[1]
    idw[own, :, NI:NI + NP] = cids_ref[...]
    ids_f = ids_i.astype(F32)
    owner = floor_div(ids_f, OWN)
    orow = floor_div(owner, C)
    ocol = owner - orow * C
    rf = r.astype(F32)
    cf = c.astype(F32)
    kslot = jnp.abs(ocol - cf) if W == 2 else ocol - cf + 1.0
    pos_f = ((orow - rf + 1.0) * W + kslot) * OWN + (ids_f - owner * OWN)
    pos = jnp.where(live, pos_f, -1.0).astype(jnp.int32)
    xw[0, own] = start_ref[...].astype(BF)

    for b in nbrs:
        def fill(b=b):
            idw[b] = jnp.full(idw.shape[1:], -1, jnp.int32)
            for s in range(ITERS):
                xw[s, b] = jnp.zeros((OWN, COLS), BF)
                rw[s, b] = jnp.zeros((OWN, COLS), BF)
            pbl[b] = jnp.zeros((NP, OWN), BF)
        unless(oks[b], fill)
    for e in (0, 1, 3, 4):
        def fill_c(e=e):
            for j in range(C):
                cw[j, e] = jnp.zeros(cw.shape[2:], BF)
        unless(row_ok5(e), fill_c)

    flat = jnp.concatenate(
        [panel_ref[a * B + b] for b in range(B) for a in range(A)], axis=0)
    pan_ref[...] = jnp.transpose(flat).astype(BF)
    cw[c, 2] = pan_ref[...]

    amount = (A - 1) + (C * B - 1)
    for e, j in far:
        ok = row_ok5(e)
        amount = amount + (1 if ok is None else ok.astype(jnp.int32))
    pl.semaphore_wait(barrier, amount)

    def send_x(s):
        send_all(lambda b: remote(
            xw.at[s, own], xw.at[s, mirror(b)], s_x.at[s, b], r_x.at[s, mirror(b)], target[b]))

    send_x(0)
    send_all(lambda b: remote(
        idw.at[own], idw.at[mirror(b)], s_id.at[b], r_id.at[mirror(b)], target[b]))

    for (e, j), dev in far.items():
        desc = remote(pan_ref, cw.at[c, 4 - e], s_w.at[e, j], r_w.at[4 - e, j], dev)
        guarded(row_ok5(e), desc.start)
        finals.append((row_ok5(e), desc.wait_send))

    pos_col = jnp.transpose(jnp.broadcast_to(pos, (128, NI)))
    WN = NB * OWN
    for j in range(0, WN, 128):
        n = min(128, WN - j)
        lane = lax.broadcasted_iota(jnp.int32, (NI, 128), 1) + j
        hot = jnp.where(lane == pos_col, 1.0, 0.0).astype(BF)
        s_ref[:, j:j + n] = hot[:, :n]
    for b in range(NB):
        sub = lax.broadcasted_iota(jnp.int32, (OWN, NI), 0) + b * OWN
        st_ref[b * OWN:(b + 1) * OWN, :] = jnp.where(sub == pos, 1.0, 0.0).astype(BF)

    def by_rows(rows, fn):
        def step(i, carry):
            fn(pl.ds(pl.multiple_of(i * OWN, OWN), OWN))
            return carry
        lax.fori_loop(0, rows // OWN, step, 0)

    def times_s(src, dst):
        def one(at):
            dst[at, :] = mm(src[at, :], s_ref[...]).astype(BF)
        by_rows(NI, one)

    def recv(dst, sem):
        return remote(dst, dst, sem, sem, (r, c)).wait_recv

    def rows_of(b):
        return slice(b * OWN, (b + 1) * OWN)

    def scatter(value, send, land, ss, rs, s):
        tv_ref[...] = value.astype(BF)
        for b in nbrs:
            send[s, b] = mm(st_ref[rows_of(b), :], tv_ref[...]).astype(BF)
            desc = remote(send.at[s, b], land.at[s, mirror(b)], ss.at[s, b],
                          rs.at[s, mirror(b)], target[b])
            guarded(oks[b], desc.start)
            finals.append((oks[b], desc.wait_send))
        tl_ref[...] = (value - tv_ref[...].astype(F32)).astype(BF)

    def own_part():
        mine = st_ref[rows_of(own), :]
        return mm(mine, tv_ref[...]) + mm(mine, tl_ref[...])

    for b in nbrs + [own]:
        block = lax.dot_general(
            basis_ref[...], st_ref[rows_of(b), :], NT, preferred_element_type=F32).astype(BF)
        if b == own:
            pbl[own] = block
        else:
            pbs[b] = block
            desc = remote(pbs.at[b], pbl.at[mirror(b)], s_b.at[b], r_b.at[mirror(b)], target[b])
            guarded(oks[b], desc.start)
            finals.append((oks[b], desc.wait_send))

    copy_k.wait()
    times_s(kv, t_ref)

    for s in range(ITERS):
        for b in nbrs:
            guarded(oks[b], recv(xw.at[s, b], r_x.at[s, b]))
        terms = loads_ref[...].astype(F32) - mm(t_ref[...], xw[s].reshape(WN, COLS))
        scatter(terms, psend, precv, s_p, r_p, s)
        r_out[...] = own_part()
        if s == 0:
            for b in nbrs:
                guarded(oks[b], recv(idw.at[b], r_id.at[b]))
            mine = lax.broadcasted_iota(jnp.int32, (OWN, 128), 0) + (r * C + c) * OWN
            acc = jnp.zeros((OWN, 128), F32)
            for b in range(NB):
                for j in range(0, NI, 128):
                    acc = acc + jnp.where(idw[b, :, j:j + 128] == mine, 1.0, 0.0)
            count = jnp.sum(acc, axis=1, keepdims=True)
            inv_ref[...] = jnp.broadcast_to(1.0 / jnp.maximum(count, 1.0), (OWN, COLS))
            copy_m.wait()
            times_s(mv, t2_ref)
            for b in nbrs:
                guarded(oks[b], recv(pbl.at[b], r_b.at[b]))
            for b in range(NB):
                first = (rf + float(b // W - 2)) * NR
                cpos = (idw[b, :, NI:NI + NP].astype(F32) - first).astype(jnp.int32)
                pt = jnp.where(
                    lax.broadcasted_iota(jnp.int32, (n_c, NP), 0) == cpos, 1.0, 0.0).astype(BF)
                block = mm(pt, pbl[b])
                pbr[b] = block.astype(BF)
                qt[b] = jnp.transpose(block).astype(BF)
        for b in nbrs:
            guarded(oks[b], recv(precv.at[s, b], r_p.at[s, b]))

            def add(b=b):
                r_out[...] = r_out[...] + precv[s, b].astype(F32)
            guarded(oks[b], add)
        z = (inv_ref[...] * r_out[...]).astype(BF)
        rw[s, own] = z
        bands = [None] * 5
        for b in range(NB):
            part = mm(pbr[b], z).reshape(3, C, NCD, COLS)
            for dd in range(3):
                e = b // W + dd
                bands[e] = part[dd] if bands[e] is None else bands[e] + part[dd]
        for e in range(5):
            csend[s, e * C:(e + 1) * C] = bands[e]
        for (e, j), dev in far.items():
            desc = remote(csend.at[s, e * C + dev[1]], crecv.at[s, 4 - e, j],
                          s_c.at[s, e, j], r_c.at[s, 4 - e, j], dev)
            guarded(row_ok5(e), desc.start)
            finals.append((row_ok5(e), desc.wait_send))
        send_all(lambda b: remote(
            rw.at[s, own], rw.at[s, mirror(b)], s_r.at[s, b], r_r.at[s, mirror(b)], target[b]))
        crecv[s, 2, 0] = csend[s, 2 * C + c]
        for e, j in far:
            guarded(row_ok5(e), recv(crecv.at[s, e, j], r_c.at[s, e, j]))

            def add_c(e=e, j=j):
                crecv[s, 2, 0] = crecv[s, 2, 0] + crecv[s, e, j]
            guarded(row_ok5(e), add_c)
        g_ref[s, c, rb, ra] = crecv[s, 2, 0].astype(BF)
        for i in range(1, A):
            at = g_ref.at[s, c, rb, ra]
            desc = remote(at, at, s_g1.at[s, i], r_g1.at[s, i], g1[i])
            desc.start()
            finals.append((None, desc.wait_send))
        for b in nbrs:
            guarded(oks[b], recv(rw.at[s, b], r_r.at[s, b]))
        scatter(mm(t2_ref[...], rw[s].reshape(WN, COLS)), usend, urecv, s_u, r_u, s)
        for i in range(1, A):
            recv(g_ref.at[s, c, rb, (ra + A - i) % A], r_g1.at[s, i])()
        for (j, i), dev in g2.items():
            if (j, i) == (0, 0):
                continue
            at = g_ref.at[s, c, rb]
            desc = remote(at, at, s_g2.at[s, j, i], r_g2.at[s, j, i], dev)
            desc.start()
            finals.append((None, desc.wait_send))
        acc_ref[...] = own_part()
        for b in nbrs:
            guarded(oks[b], recv(urecv.at[s, b], r_u.at[s, b]))

            def add_u(b=b):
                acc_ref[...] = acc_ref[...] + urecv[s, b].astype(F32)
            guarded(oks[b], add_u)
        for (j, i) in g2:
            if (j, i) == (0, 0):
                continue
            recv(g_ref.at[s, (c + C - j) % C, (rb + B - i) % B], r_g2.at[s, j, i])()
        if s == 0:
            for e, j in far:
                guarded(row_ok5(e), recv(cw.at[(c + C - j) % C, e], r_w.at[e, j]))
        sol = None
        for j in range(C):
            rhs = g_ref[s, j].astype(F32).reshape(R * NCD, COLS).astype(BF)
            term = mm(cw[j].reshape(5 * NR, R * NCD), rhs)
            sol = term if sol is None else sol + term
        sol = sol.astype(BF)
        total = acc_ref[...]
        for b in range(NB):
            d = b // W
            total = total + mm(qt[b], sol[d * NR:(d + 3) * NR])
        x_now = (start_ref if s == 0 else x_out)[...] + inv_ref[...] * total
        x_out[...] = x_now
        if s + 1 < ITERS:
            xw[s + 1, own] = x_now.astype(BF)
            send_x(s + 1)
    for ok, fn in finals:
        guarded(ok, fn)


def hand_over(x_in, r_in, x_out, r_out):
    x_out[...] = x_in[...]
    r_out[...] = r_in[...]


def solution(mesh):
    R, C = mesh.shape["row"], mesh.shape["col"]
    B = 4 if R % 4 == 0 else (2 if R % 2 == 0 else 1)
    A = R // B
    W = 2 if C == 2 else 3
    NB = 3 * W

    def body(stiffness, local_inverse, averaging_basis, loads, start, coarse_inverse, sizes,
             dof_ids, coarse_ids):
        OWN, COLS = start.shape
        NI = dof_ids.shape[1]
        NCD, NR = coarse_inverse.shape[2:]
        WN = NB * OWN
        panel = coarse_inverse.reshape(R, NCD, NR)
        V = pltpu.VMEM
        D = pltpu.SemaphoreType.DMA
        S = ITERS
        vm = pl.BlockSpec(memory_space=pltpu.VMEM)
        hb = pl.BlockSpec(memory_space=pl.ANY)
        sm = pl.BlockSpec(memory_space=pltpu.SMEM)
        n_c = 3 * NR
        NP = coarse_ids.shape[1]
        pair = pl.pallas_call(
            functools.partial(kernel, R, C, B),
            out_shape=(jax.ShapeDtypeStruct((OWN, COLS), F32),) * 2,
            in_specs=[hb, hb, vm, vm, vm, vm, sm, vm, vm],
            out_specs=(vm, vm),
            scratch_shapes=[
                V((NI, NI), BF), V((NI, NI), BF), V((NI, WN), BF), V((WN, NI), BF),
                V((NI, WN), BF), V((NI, WN), BF), V((NI, COLS), BF), V((NI, COLS), BF),
                V((NB, NP, OWN), BF), V((NB, NP, OWN), BF),
                V((NB, n_c, OWN), BF), V((NB, OWN, n_c), BF),
                V((NB, 1, NI + 128 * pl.cdiv(NP, 128)), jnp.int32), V((S, NB, OWN, COLS), BF), V((S, NB, OWN, COLS), BF),
                V((S, NB, OWN, COLS), BF), V((S, NB, OWN, COLS), BF),
                V((S, NB, OWN, COLS), BF), V((S, NB, OWN, COLS), BF),
                V((S, 5 * C, NCD, COLS), F32), V((S, 5, C, NCD, COLS), F32),
                V((C, 5, NR, R * NCD), BF), V((NR, R * NCD), BF),
                V((S, C, B, A, NCD, COLS), BF),
                V((OWN, COLS), F32), V((OWN, COLS), F32),
                D((2,)), D((NB,)), D((NB,)), D((S, NB)), D((S, NB)), D((S, NB)), D((S, NB)),
                D((S, NB)), D((S, NB)), D((S, NB)), D((S, NB)), D((NB,)), D((NB,)),
                D((S, 5, C)), D((S, 5, C)), D((5, C)), D((5, C)),
                D((S, A)), D((S, A)), D((S, C, B)), D((S, C, B)),
            ],
            compiler_params=pltpu.CompilerParams(
                collective_id=0, has_side_effects=True, vmem_limit_bytes=62 << 20
            ),
        )(stiffness[0], local_inverse[0], jnp.swapaxes(averaging_basis[0], 0, 1), loads[0], start, panel, sizes,
          dof_ids, coarse_ids)
        return pl.pallas_call(
            hand_over,
            out_shape=(jax.ShapeDtypeStruct((OWN, COLS), F32),) * 2,
            in_specs=[vm, vm],
            out_specs=(vm, vm),
        )(*pair)

    in_specs = (
        P(("row", "col"), None, None),
        P(("row", "col"), None, None),
        P(("row", "col"), None, None),
        P(("row", "col"), None, None),
        P(("row", "col"), None),
        P(None, "col", None, "row"),
        P(("row", "col")),
        P(("row", "col"), None),
        P(("row", "col"), None),
    )
    out_specs = (P(("row", "col"), None), P(("row", "col"), None))
    return jax.shard_map(body, mesh=mesh, in_specs=in_specs, out_specs=out_specs, check_vma=False)
```
